32 devices in a mesh: ctx: 8 (over z, y), head: 4 (over x, core).
Axes of the slice: x: 2, y: 2, z: 4, core: 2. Of those that a mesh axis runs over, the one named last changes fastest.
Arguments:
- queries: bfloat16 [4096, 2048], P(('ctx', 'head')), may hold values from -6 to 6
- key_rows: bfloat16 [4096, 256], P(('ctx', 'head')), may hold values from -6 to 6
- value_rows: bfloat16 [4096, 256], P(('ctx', 'head')), may hold values from -8 to 8
- group_kv_head: int32 [4], replicated, may hold values from 0 to 1, as said below
- doc_ids: int32 [4096], replicated, may hold values from 0 to 127, never falling along the last dimension, each value on 1 to 64 neighbouring positions
Outputs:
- attended: bfloat16 [4096, 2048], P(('ctx', 'head'))
The draws below stay inside these ranges and needn't reach their ends.
Inputs may be any that keep to these rules, and one draw needn't show every extreme that they name: `group_kv_head`: each key-value head is named by exactly two groups. `doc_ids`: ids never fall along the sequence and every id appears; a document holds at most 64 tokens, and one holds exactly that many.
All inputs are finite; a program needn't handle non-finite values.
Results may differ from the reference program's by a relative error of at most 0.0027.
Values may be sent and summed in bfloat16 or wider, within the bound.
No kernel may reach another device: no remote copies, remote signals or barrier semaphores. Data moves between devices by JAX's collectives and lax.ppermute only.
A program may use at most 64 MiB of HBM per device.

```python
import math
import jax
import jax.numpy as jnp
import numpy as np
from jax import lax

HEAD_DIM = 128
HEADS_DEV = 4
TOK_DEV = 512
QUERY_HEADS = 16
KV_HEADS = 2
GROUPS = 4
TOKENS = 4096
DOCS = 128


def draw_queries(key, part):
    base = 1.4 * jax.random.normal(jax.random.fold_in(key, 11), (TOKENS, QUERY_HEADS * HEAD_DIM), jnp.float32)
    base = jnp.clip(base, -6.0, 6.0)
    return base.astype(jnp.bfloat16)


def draw_key_rows(key, part):
    base = 1.4 * jax.random.normal(jax.random.fold_in(key, 17), (TOKENS, KV_HEADS * HEAD_DIM), jnp.float32)
    base = jnp.clip(base, -6.0, 6.0)
    return base.astype(jnp.bfloat16)


def draw_group_kv_head(key, part):
    return (jax.random.permutation(jax.random.fold_in(key, 23), GROUPS) // 2).astype(jnp.int32)


def steps_of(stream_key, dims, shards, least, top_value):
    level, own = 1.0, jax.random.fold_in(stream_key, 6)
    for dim, blocks in shards:
        draws = jnp.exp(jax.random.uniform(jax.random.fold_in(own, dim), (blocks,), jnp.float32, least / len(shards), top_value / len(shards)))
        level = level * jnp.repeat(draws, dims[dim] // blocks).reshape([-1 if axis == dim else 1 for axis in range(len(dims))])
    return level


def length_profile(number_of, total, most, lean):
    portions = [(1 << 20) // math.isqrt(standing ** lean) + 1 for standing in range(2, number_of + 1)]
    spare, counts = total - most - (number_of - 1), [1] * (number_of - 1)
    while spare > 0:
        free = [i for i in range(number_of - 1) if counts[i] < most]
        pool, budget = sum([portions[i] for i in free]), spare
        for i in free:
            addition = min(most - counts[i], max(1, budget * portions[i] // pool), spare)
            counts[i] = counts[i] + addition
            spare = spare - addition
    return np.array([most] + counts)


def uneven(key, count, total, most, slope):
    if count == 2:
        one = jax.random.randint(key, (), max(1, total - most), min(most, total - 1) + 1)
        return jnp.stack([one, total - one])
    lengths = jnp.asarray(length_profile(count, total, most, slope), jnp.int32)
    couples = (count - 1) // 2
    source_of, sink = lengths[1:1 + 2 * couples:2], lengths[2:2 + 2 * couples:2]
    slack = jnp.minimum(source_of - 1, most - sink)
    shifted = jax.random.randint(jax.random.fold_in(key, 1), (couples,), 0, 1 << 20) % (slack + 1)
    lengths = lengths.at[1:1 + 2 * couples:2].set(source_of - shifted).at[2:2 + 2 * couples:2].set(sink + shifted)
    return lengths[jax.random.permutation(jax.random.fold_in(key, 2), count)]


def bell_draw(stream_key, extent, spread, bound, split=(), held_as=jnp.bfloat16):
    values = spread * jax.random.normal(stream_key, extent, jnp.float32)
    if split:
        values = values * steps_of(stream_key, extent, split, -0.22, 0.18)
    return jnp.clip(values, -bound, bound).astype(held_as)


def setup_inputs(seed: int = 0) -> dict:
    key_list = jax.random.split(jax.random.key(seed), 6)
    return {
        "queries": draw_queries(jax.random.fold_in(key_list[5], 71), 0),
        "key_rows": draw_key_rows(jax.random.fold_in(key_list[5], 71), 0),
        "value_rows": bell_draw(key_list[2], (TOKENS, KV_HEADS * HEAD_DIM), 2.0, 8.0, ((0, 32),)),
        "group_kv_head": draw_group_kv_head(jax.random.fold_in(key_list[5], 71), 0),
        "doc_ids": jnp.searchsorted(jnp.cumsum(uneven(key_list[4], DOCS, TOKENS, TOK_DEV // 8, 1)), jnp.arange(TOKENS), side="right").astype(jnp.int32),
    }


def reference(queries, key_rows, value_rows, group_kv_head, doc_ids):
    scale_factor = 1.0 / math.sqrt(HEAD_DIM)
    block_rows = TOK_DEV // 16
    reach = TOK_DEV // 8
    window = reach + block_rows
    block_count = TOKENS // block_rows
    query_heads = queries.reshape(TOKENS, QUERY_HEADS, HEAD_DIM).transpose(1, 0, 2)
    key_pad = jnp.concatenate([jnp.zeros((reach, KV_HEADS * HEAD_DIM), jnp.bfloat16), key_rows], axis=0)
    value_pad = jnp.concatenate([jnp.zeros((reach, KV_HEADS * HEAD_DIM), jnp.bfloat16), value_rows], axis=0)
    key_heads = key_pad.reshape(TOKENS + reach, KV_HEADS, HEAD_DIM).transpose(1, 0, 2)
    value_heads = value_pad.reshape(TOKENS + reach, KV_HEADS, HEAD_DIM).transpose(1, 0, 2)
    doc_pad = jnp.concatenate([jnp.full((reach,), -1, jnp.int32), doc_ids.astype(jnp.int32)], axis=0)
    head_source = jnp.repeat(group_kv_head, HEADS_DEV).astype(jnp.int32)

    def one_head(inputs):
        query_head, source = inputs
        key_head = key_heads[source]
        value_head = value_heads[source]

        def one_block(block_index):
            start = (block_index * block_rows).astype(jnp.int32)
            query_block = lax.dynamic_slice_in_dim(query_head, start, block_rows, 0)
            key_block = lax.dynamic_slice_in_dim(key_head, start, window, 0)
            value_block = lax.dynamic_slice_in_dim(value_head, start, window, 0)
            key_doc = lax.dynamic_slice_in_dim(doc_pad, start, window, 0)
            query_doc = lax.dynamic_slice_in_dim(doc_ids.astype(jnp.int32), start, block_rows, 0)
            query_pos = start + jnp.arange(block_rows, dtype=jnp.int32)
            key_pos = start - reach + jnp.arange(window, dtype=jnp.int32)
            scores = jnp.dot(query_block, key_block.T, preferred_element_type=jnp.float32) * scale_factor
            visible = (key_pos[None, :] <= query_pos[:, None]) & (key_doc[None, :] == query_doc[:, None])
            scores = jnp.where(visible, scores, -1e+30)
            row_peak = lax.optimization_barrier(jnp.max(scores, axis=1, keepdims=True))
            expo = jnp.where(visible, jnp.exp(scores - row_peak), 0.0)
            totals = lax.optimization_barrier(jnp.sum(expo, axis=1, keepdims=True))
            weights = expo.astype(jnp.bfloat16)
            mixed = jnp.dot(weights, value_block, preferred_element_type=jnp.float32)
            return (mixed / totals).astype(jnp.bfloat16)
        blocks = lax.map(one_block, jnp.arange(block_count, dtype=jnp.int32))
        return blocks.reshape(TOKENS, HEAD_DIM)
    outputs = lax.map(one_head, (query_heads, head_source))
    return outputs.transpose(1, 0, 2).reshape(TOKENS, QUERY_HEADS * HEAD_DIM)
```

```python
import functools
import math

import jax
import jax.numpy as jnp
from jax import lax
from jax.experimental import pallas as pl
from jax.experimental.pallas import tpu as pltpu
from jax.sharding import PartitionSpec as P

HEAD_DIM = 128
HEADS_DEV = 4
WIDTH = HEADS_DEV * HEAD_DIM
AXES = ("ctx", "head")
neg_fill = -1e30
FACTOR = math.log2(math.e) / math.sqrt(HEAD_DIM)


def flat_index():
    return lax.axis_index("ctx") * lax.axis_size("head") + lax.axis_index("head")


def bias_of(visible):
    return jnp.where(visible, 0.0, neg_fill)


def attend_group(query, key, value, bias):
    stack = query.shape[0] // bias.shape[0]
    scores = lax.dot_general(query, key, (((1,), (1,)), ((), ())), preferred_element_type=jnp.float32)
    scores = scores * FACTOR + jnp.concatenate([bias] * stack, axis=0)
    peak = jnp.max(scores, axis=1, keepdims=True)
    expo = jnp.exp2(scores - peak)
    totals = jnp.sum(expo, axis=1, keepdims=True)
    mixed = jnp.dot(expo.astype(jnp.bfloat16), value, preferred_element_type=jnp.float32)
    return (mixed / totals).astype(jnp.bfloat16)


def column_of(row):
    return jnp.transpose(jnp.broadcast_to(row, (row.shape[1], row.shape[1])))


def head_stack(ref, rows, g):
    return jnp.concatenate(
        [ref[rows, g * WIDTH + h * HEAD_DIM:g * WIDTH + (h + 1) * HEAD_DIM] for h in range(HEADS_DEV)], axis=0)


def store_heads(ref, g, result):
    n = result.shape[0] // HEADS_DEV
    for h in range(HEADS_DEV):
        ref[:, g * WIDTH + h * HEAD_DIM:g * WIDTH + (h + 1) * HEAD_DIM] = result[h * n:(h + 1) * n]


def send_out(buf, out_ref, first, g, sem):
    cols = pl.ds(g * WIDTH, WIDTH)
    return pltpu.make_async_copy(buf.at[:, cols], out_ref.at[pl.ds(first, buf.shape[0]), cols], sem.at[g])


def inner_kernel(reach, hops, group_ref, doc_ref, q_ref, k_ref, v_ref, out_ref, bias_ref, local_ref, pick_ref, *scratch):
    rows, groups, kv_count = q_ref.shape[0], q_ref.shape[1] // WIDTH, k_ref.shape[1] // HEAD_DIM
    near = min(reach, rows)
    me = flat_index()
    own = doc_ref[pl.ds(me, 1), :]
    col = column_of(own)
    t = lax.broadcasted_iota(jnp.int32, (rows, rows), 0)
    u = lax.broadcasted_iota(jnp.int32, (rows, rows), 1)
    before = [doc_ref[pl.ds(jnp.maximum(me - j, 0), 1), :] for j in range(1, hops + 1)]
    own_bias = bias_of((own == col) & (u <= t))
    if near < rows:
        docs = jnp.where(u < near, own, before[0])
        pos = jnp.where(u < near, u, u - rows)
        bias_ref[...] = bias_of((docs == col) & (pos <= t) & (pos + me * rows >= 0))[:near]
    else:
        bias_ref[...] = jnp.concatenate(
            [own_bias] + [bias_of((before[j] == col) & (u + (me - 1 - j) * rows >= 0)) for j in range(hops)], axis=1)
    for g in range(groups):
        c = pl.ds(pl.multiple_of(group_ref[g] * HEAD_DIM, HEAD_DIM), HEAD_DIM)
        local_ref[g, :, :HEAD_DIM] = k_ref[:near, c]
        local_ref[g, :, HEAD_DIM:] = v_ref[:near, c]
        for j in range(kv_count):
            pick_ref[g * kv_count + j] = jnp.full((16, HEAD_DIM), jnp.where(group_ref[g] == j, 1.0, 0.0)).astype(jnp.bfloat16)
    if near < rows:
        buf, sem = scratch
        for g in range(groups):
            c = pl.ds(pl.multiple_of(group_ref[g] * HEAD_DIM, HEAD_DIM), HEAD_DIM)
            store_heads(buf, g, attend_group(head_stack(q_ref, slice(near, rows), g), k_ref[:, c], v_ref[:, c], own_bias[near:]))
            send_out(buf, out_ref, near, g, sem).start()
        for g in range(groups):
            send_out(buf, out_ref, near, g, sem).wait()


def picked(rim, pick_ref, g, kv_count, first):
    parts = []
    for j in range(kv_count):
        at = first + j * HEAD_DIM
        part = rim[:, at:at + HEAD_DIM]
        parts.append(part * jnp.concatenate([pick_ref[g * kv_count + j]] * (part.shape[0] // 16), axis=0))
    return functools.reduce(jnp.add, parts)


def rim_kernel(q_ref, bias_ref, local_ref, pick_ref, *refs):
    *rim_refs, _, out_ref, buf, sem = refs
    near, groups = local_ref.shape[1], q_ref.shape[1] // WIDTH
    kv_count = pick_ref.shape[0] // groups
    width = kv_count * HEAD_DIM
    odd = flat_index() % 2 == 1
    if near < q_ref.shape[0]:
        even_ref, odd_ref = rim_refs
        rims = [jnp.where(odd, odd_ref[...], even_ref[...])]
    else:
        rims = [r[...] for r in rim_refs]
    for g in range(groups):
        key = jnp.concatenate([local_ref[g, :, :HEAD_DIM]] + [picked(r, pick_ref, g, kv_count, 0) for r in rims], axis=0)
        value = jnp.concatenate([local_ref[g, :, HEAD_DIM:]] + [picked(r, pick_ref, g, kv_count, width) for r in rims], axis=0)
        store_heads(buf, g, attend_group(head_stack(q_ref, slice(0, near), g), key, value, bias_ref[...]))
        send_out(buf, out_ref, 0, g, sem).start()
    for g in range(groups):
        send_out(buf, out_ref, 0, g, sem).wait()


SMEM = pl.BlockSpec(memory_space=pltpu.SMEM)
VMEM = pl.BlockSpec(memory_space=pltpu.VMEM)
ANY = pl.BlockSpec(memory_space=pl.ANY)


def crossings(devices):
    last = devices - 1
    pairs = [(i, i + 1) for i in range(1, last, 2)]
    pairs += [(i, i - 1) for i in range(4, last - 1, 2)]
    return pairs + [(0, 1), (2, 0), (last - 1, last), (last, last - 2)]


def on_device(queries, key_rows, value_rows, group_kv_head, doc_ids):
    rows = queries.shape[0]
    devices = lax.axis_size("ctx") * lax.axis_size("head")
    groups, kv_count = queries.shape[1] // WIDTH, key_rows.shape[1] // HEAD_DIM
    reach = rows * lax.axis_size("head") // 8
    near = min(reach, rows)
    hops = -(-reach // rows)
    docs = doc_ids.reshape(devices, rows)
    edge = jnp.concatenate([key_rows[rows - near:], value_rows[rows - near:]], axis=1)
    if near < rows:
        rims = [lax.ppermute(edge, AXES, crossings(devices)),
                lax.ppermute(edge, AXES, [(i, i ^ 1) for i in range(devices)])]
    else:
        rims = [lax.ppermute(edge, AXES, [(i, i + j) for i in range(devices - j)]) for j in range(1, hops + 1)]
    small = near < rows
    vmem = lambda x: pltpu.with_memory_space_constraint(x, pltpu.VMEM) if small else x
    chip = pltpu.VMEM if small else jax.ShapeDtypeStruct
    keys = 2 * near if near < rows else rows * (1 + hops)
    buf = [pltpu.VMEM((rows - near, queries.shape[1]), queries.dtype), pltpu.SemaphoreType.DMA((groups,))]
    q = vmem(queries)
    partial, bias, local, pick = pl.pallas_call(
        functools.partial(inner_kernel, reach, hops),
        out_shape=[
            pltpu.HBM(queries.shape, queries.dtype),
            chip((near, keys), jnp.float32),
            chip((groups, near, 2 * HEAD_DIM), key_rows.dtype),
            chip((groups * kv_count, 16, HEAD_DIM), key_rows.dtype),
        ],
        in_specs=[SMEM] + [VMEM] * 4, out_specs=[ANY] + [VMEM] * 3, name="inner",
        scratch_shapes=buf if near < rows else [],
    )(group_kv_head, docs, q, vmem(key_rows), vmem(value_rows))
    return pl.pallas_call(
        rim_kernel, out_shape=jax.ShapeDtypeStruct(queries.shape, queries.dtype),
        in_specs=[VMEM] * (4 + len(rims)) + [ANY], out_specs=ANY, name="rim",
        scratch_shapes=[pltpu.VMEM((near, queries.shape[1]), queries.dtype), pltpu.SemaphoreType.DMA((groups,))],
        input_output_aliases={4 + len(rims): 0},
    )(q, vmem(bias), vmem(local), vmem(pick), *[vmem(r) for r in rims], partial)


def solution(mesh):
    placed = P(AXES, None)
    return jax.shard_map(
        on_device, mesh=mesh, in_specs=(placed, placed, placed, P(), P()), out_specs=placed, check_vma=False
    )
```

```python
import functools
import math

import jax
import jax.numpy as jnp
from jax import lax
from jax.experimental import pallas as pl
from jax.experimental.pallas import tpu as pltpu
from jax.sharding import PartitionSpec as P

HEAD_DIM = 128
HEADS_DEV = 4
WIDTH = HEADS_DEV * HEAD_DIM
AXES = ("ctx", "head")
neg_fill = -1e30
FACTOR = math.log2(math.e) / math.sqrt(HEAD_DIM)


def flat_index():
    return lax.axis_index("ctx") * lax.axis_size("head") + lax.axis_index("head")


def bias_of(visible):
    bias = jnp.where(visible, 0.0, neg_fill)
    return jnp.concatenate([bias] * HEADS_DEV, axis=1)


def attend_group(query, key, value, bias):
    scores = lax.dot_general(key, query, (((1,), (1,)), ((), ())), preferred_element_type=jnp.float32)
    scores = scores * FACTOR + bias
    expo = jnp.exp2(scores - jnp.max(scores, axis=0, keepdims=True))
    inverse = 1.0 / jnp.sum(expo, axis=0, keepdims=True)
    mixed = lax.dot_general(
        value, expo.astype(jnp.bfloat16), (((0,), (0,)), ((), ())), preferred_element_type=jnp.float32)
    return jnp.transpose((mixed * inverse).astype(jnp.bfloat16))


def column_of(row):
    return jnp.transpose(jnp.broadcast_to(row, (row.shape[1], row.shape[1])))


def head_stack(ref, g):
    return jnp.concatenate(
        [ref[:, g * WIDTH + h * HEAD_DIM:g * WIDTH + (h + 1) * HEAD_DIM] for h in range(HEADS_DEV)], axis=0)


def store_heads(ref, g, result):
    n = result.shape[0] // HEADS_DEV
    for h in range(HEADS_DEV):
        ref[:, g * WIDTH + h * HEAD_DIM:g * WIDTH + (h + 1) * HEAD_DIM] = result[h * n:(h + 1) * n]


def send_out(buf, out_ref, first, g, sem):
    cols = pl.ds(g * WIDTH, WIDTH)
    return pltpu.make_async_copy(buf.at[:, cols], out_ref.at[pl.ds(first, buf.shape[0]), cols], sem.at[g])


def inner_kernel(near, hops, group_hbm, doc_hbm, q_hbm, k_hbm, v_hbm, out_ref, near_ref, bias_ref, local_ref, pick_ref,
                 group_ref, doc_ref, k_ref, v_ref, load_sem, *scratch):
    rows, groups, kv_count = q_hbm.shape[0], q_hbm.shape[1] // WIDTH, k_hbm.shape[1] // HEAD_DIM
    loads = [(doc_hbm, doc_ref), (group_hbm, group_ref), (k_hbm, k_ref), (v_hbm, v_ref)]
    if near < rows:
        q_ref, buf, sem = scratch
        loads.append((q_hbm.at[pl.ds(near, rows - near)], q_ref))
    loads.append((q_hbm.at[pl.ds(0, near)], near_ref))
    loads = [pltpu.make_async_copy(a, b, load_sem.at[i]) for i, (a, b) in enumerate(loads)]
    for load in loads:
        load.start()
    me = flat_index()
    loads[0].wait()
    own = doc_ref[pl.ds(me, 1), :]
    before = [doc_ref[pl.ds(jnp.maximum(me - j, 0), 1), :] for j in range(1, hops + 1)]
    u = lax.broadcasted_iota(jnp.int32, (rows, rows), 0)
    t = lax.broadcasted_iota(jnp.int32, (rows, rows), 1)
    own_seen = (column_of(own) == own) & (u <= t)
    if near < rows:
        docs = column_of(jnp.where(lax.broadcasted_iota(jnp.int32, own.shape, 1) < near, own, before[0]))
        pos = jnp.where(u < near, u, u - rows)
        bias_ref[...] = bias_of(((docs == own) & (pos <= t) & (pos + me * rows >= 0))[:, :near])
    else:
        bias_ref[...] = jnp.concatenate(
            [bias_of(own_seen)]
            + [bias_of((column_of(before[j]) == own) & (u + (me - 1 - j) * rows >= 0)) for j in range(hops)], axis=0)
    for load in loads[1:4]:
        load.wait()
    for g in range(groups):
        c = pl.ds(pl.multiple_of(group_ref[g] * HEAD_DIM, HEAD_DIM), HEAD_DIM)
        local_ref[g, :, :HEAD_DIM] = k_ref[:near, c]
        local_ref[g, :, HEAD_DIM:] = v_ref[:near, c]
        for j in range(kv_count):
            pick_ref[g * kv_count + j] = jnp.full((16, HEAD_DIM), jnp.where(group_ref[g] == j, 1.0, 0.0)).astype(jnp.bfloat16)
    for load in loads[4:]:
        load.wait()
    if near < rows:
        bias = bias_of(own_seen[:, near:])
        for g in range(groups):
            c = pl.ds(pl.multiple_of(group_ref[g] * HEAD_DIM, HEAD_DIM), HEAD_DIM)
            store_heads(buf, g, attend_group(head_stack(q_ref, g), k_ref[:, c], v_ref[:, c], bias))
            send_out(buf, out_ref, near, g, sem).start()
        for g in range(groups):
            send_out(buf, out_ref, near, g, sem).wait()


def picked(rim, pick_ref, g, kv_count, first):
    parts = []
    for j in range(kv_count):
        part = rim[:, first + j * HEAD_DIM:first + (j + 1) * HEAD_DIM]
        parts.append(part * jnp.concatenate([pick_ref[g * kv_count + j]] * (part.shape[0] // 16), axis=0))
    return functools.reduce(jnp.add, parts)


def rim_kernel(period, q_ref, bias_ref, local_ref, pick_ref, *refs):
    *rim_refs, _, out_ref, buf, sem = refs
    groups = q_ref.shape[1] // WIDTH
    kv_count = pick_ref.shape[0] // groups
    width = kv_count * HEAD_DIM
    if period:
        me = flat_index()
        swap = (me % period == 1) & (me > 1)
        rims = [jnp.where(swap, rim_refs[1][...], rim_refs[0][...])]
    else:
        rims = [r[...] for r in rim_refs]
    for g in range(groups):
        key = jnp.concatenate([local_ref[g, :, :HEAD_DIM]] + [picked(r, pick_ref, g, kv_count, 0) for r in rims], axis=0)
        value = jnp.concatenate([local_ref[g, :, HEAD_DIM:]] + [picked(r, pick_ref, g, kv_count, width) for r in rims], axis=0)
        store_heads(buf, g, attend_group(head_stack(q_ref, g), key, value, bias_ref[...]))
        send_out(buf, out_ref, 0, g, sem).start()
    for g in range(groups):
        send_out(buf, out_ref, 0, g, sem).wait()


VMEM = pl.BlockSpec(memory_space=pltpu.VMEM)
ANY = pl.BlockSpec(memory_space=pl.ANY)


def cycles(devices, period):
    firsts = [0] + [m + 1 for m in range(period, devices, period)] + [devices]
    pairs = []
    for a, b in zip(firsts, firsts[1:]):
        pairs += [(i, i + 1) for i in range(a, b - 1)] + [(b - 1, a)]
    return pairs


def on_device(queries, key_rows, value_rows, group_kv_head, doc_ids):
    rows = queries.shape[0]
    devices = lax.axis_size("ctx") * lax.axis_size("head")
    period = 2 * lax.axis_size("head")
    groups, kv_count = queries.shape[1] // WIDTH, key_rows.shape[1] // HEAD_DIM
    reach = rows * lax.axis_size("head") // 8
    near = min(reach, rows)
    hops = -(-reach // rows)
    small = near < rows
    docs = doc_ids.reshape(devices, rows)
    edge = jnp.concatenate([key_rows[rows - near:], value_rows[rows - near:]], axis=1)
    if small:
        rims = [lax.ppermute(edge, AXES, cycles(devices, period)),
                lax.ppermute(edge, AXES, [(i, i ^ 1) for i in range(devices)])]
    else:
        rims = [lax.ppermute(edge, AXES, [(i, i + j) for i in range(devices - j)]) for j in range(1, hops + 1)]
    vmem = lambda x: pltpu.with_memory_space_constraint(x, pltpu.VMEM) if small else x
    chip = pltpu.VMEM if small else jax.ShapeDtypeStruct
    keys = 2 * near if small else rows * (1 + hops)
    dtype = queries.dtype
    partial, near_q, bias, local, pick = pl.pallas_call(
        functools.partial(inner_kernel, near, hops),
        out_shape=[
            pltpu.HBM(queries.shape, dtype),
            chip((near, queries.shape[1]), dtype),
            chip((keys, HEADS_DEV * near), jnp.float32),
            chip((groups, near, 2 * HEAD_DIM), dtype),
            chip((groups * kv_count, 16, HEAD_DIM), dtype),
        ],
        in_specs=[ANY] * 5, out_specs=[ANY] + [VMEM] * 4, name="inner",
        scratch_shapes=[
            pltpu.SMEM(group_kv_head.shape, jnp.int32), pltpu.VMEM(docs.shape, jnp.int32),
            pltpu.VMEM(key_rows.shape, dtype), pltpu.VMEM(key_rows.shape, dtype), pltpu.SemaphoreType.DMA((6,)),
        ] + ([pltpu.VMEM((rows - near, queries.shape[1]), dtype)] * 2 + [pltpu.SemaphoreType.DMA((groups,))] if small else []),
    )(group_kv_head, docs, queries, key_rows, value_rows)
    return pl.pallas_call(
        functools.partial(rim_kernel, period if small else 0),
        out_shape=jax.ShapeDtypeStruct(queries.shape, dtype),
        in_specs=[VMEM] * (4 + len(rims)) + [ANY], out_specs=ANY, name="rim",
        scratch_shapes=[pltpu.VMEM((near, queries.shape[1]), dtype), pltpu.SemaphoreType.DMA((groups,))],
        input_output_aliases={4 + len(rims): 0},
    )(*[vmem(x) for x in (near_q, bias, local, pick, *rims)], partial)


def solution(mesh):
    placed = P(AXES, None)
    return jax.shard_map(
        on_device, mesh=mesh, in_specs=(placed, placed, placed, P(), P()), out_specs=placed, check_vma=False
    )
```

```python
import functools
import math

import jax
import jax.numpy as jnp
from jax import lax
from jax.experimental import pallas as pl
from jax.experimental.pallas import tpu as pltpu
from jax.sharding import PartitionSpec as P


HEAD_DIM = 128
HEADS_DEV = 4
WIDTH = HEADS_DEV * HEAD_DIM
AXES = ("ctx", "head")
neg_fill = -1e30
FACTOR = math.log2(math.e) / math.sqrt(HEAD_DIM)


def flat_index():
    return lax.axis_index("ctx") * lax.axis_size("head") + lax.axis_index("head")


def bias_of(visible):
    return jnp.where(visible, 0.0, neg_fill)


def scores_of(query, key, bias):
    raw = lax.dot_general(query, key, (((1,), (1,)), ((), ())), preferred_element_type=jnp.float32)
    return raw * FACTOR + jnp.concatenate([bias] * HEADS_DEV, axis=0)


def softmax_parts(scores):
    expo = jnp.exp2(scores - jnp.max(scores, axis=1, keepdims=True))
    inverse = 1.0 / jnp.sum(expo, axis=1, keepdims=True)
    return expo.astype(jnp.bfloat16), inverse


def mix(weights, inverse, value):
    return (jnp.dot(weights, value, preferred_element_type=jnp.float32) * inverse).astype(jnp.bfloat16)


def column_of(row):
    return jnp.transpose(jnp.broadcast_to(row, (row.shape[1], row.shape[1])))


def head_stack(ref, g):
    return jnp.concatenate(
        [ref[:, g * WIDTH + h * HEAD_DIM:g * WIDTH + (h + 1) * HEAD_DIM] for h in range(HEADS_DEV)], axis=0)


def store_heads(ref, g, result):
    n = result.shape[0] // HEADS_DEV
    for h in range(HEADS_DEV):
        ref[:, g * WIDTH + h * HEAD_DIM:g * WIDTH + (h + 1) * HEAD_DIM] = result[h * n:(h + 1) * n]


def send_out(buf, out_ref, first, g, sem):
    cols = pl.ds(g * WIDTH, WIDTH)
    return pltpu.make_async_copy(buf.at[:, cols], out_ref.at[pl.ds(first, buf.shape[0]), cols], sem.at[g])


def columns(group_ref, g, offset=0):
    return pl.ds(pl.multiple_of(group_ref[g] * HEAD_DIM + offset, HEAD_DIM), HEAD_DIM)


def inner_kernel(near, hops, group_hbm, doc_hbm, q_hbm, k_hbm, v_hbm, group_ref, near_q, near_k, near_v, bias_ref, *refs):
    rows, groups = q_hbm.shape[0], q_hbm.shape[1] // WIDTH
    *done, names_ref, doc_ref, k_ref, v_ref, load_sem = refs[:-1] if near < rows else refs
    loads = [(doc_hbm, doc_ref), (k_hbm, k_ref), (group_hbm, names_ref), (v_hbm, v_ref)]
    if near < rows:
        q_ref = refs[-1]
        loads.append((q_hbm.at[pl.ds(near, rows - near)], q_ref))
    loads.append((q_hbm.at[pl.ds(0, near)], near_q))
    loads = [pltpu.make_async_copy(a, b, load_sem.at[i]) for i, (a, b) in enumerate(loads)]
    for load in loads:
        load.start()
    me = flat_index()
    loads[0].wait()
    own = doc_ref[pl.ds(me, 1), :]
    before = [doc_ref[pl.ds(jnp.maximum(me - j, 0), 1), :] for j in range(1, hops + 1)]
    col = column_of(own)
    t = lax.broadcasted_iota(jnp.int32, (rows, rows), 0)
    u = lax.broadcasted_iota(jnp.int32, (rows, rows), 1)
    own_bias = bias_of((own == col) & (u <= t))
    if near < rows:
        docs = jnp.where(u < near, own, before[0])
        pos = jnp.where(u < near, u, u - rows)
        bias_ref[...] = bias_of((docs == col) & (pos <= t) & (pos + me * rows >= 0))[:near]
    else:
        bias_ref[...] = jnp.concatenate(
            [own_bias] + [bias_of((before[j] == col) & (u + (me - 1 - j) * rows >= 0)) for j in range(hops)], axis=1)
    for load in loads[1:]:
        load.wait()
    for g in range(groups):
        group_ref[g] = names_ref[g]
    near_k[...] = k_ref[:near]
    near_v[...] = v_ref[:near]
    if near < rows:
        for g in range(groups):
            c = columns(names_ref, g)
            store_heads(
                done[0], g, mix(*softmax_parts(scores_of(head_stack(q_ref, g), k_ref[:, c], own_bias[near:])), v_ref[:, c]))


def with_rim(near_ref, rims, heads, group_ref, g, offset):
    near, here = near_ref.shape[0], columns(group_ref, g)
    if heads:
        me = flat_index()
        swap = functools.reduce(jnp.logical_or, [me == head for head in heads])
        main, side = (r[r.shape[0] - near:, here] for r in rims)
        parts = [jnp.where(swap, side, main)]
    else:
        parts = [r[:, columns(group_ref, g, offset)] for r in rims]
    return jnp.concatenate([near_ref[:, here]] + parts, axis=0)


def weight_kernel(heads, group_ref, q_ref, bias_ref, k_ref, *refs):
    *rims, weight_ref, inverse_ref = refs
    groups = q_ref.shape[1] // WIDTH
    scores = [
        scores_of(head_stack(q_ref, g), with_rim(k_ref, rims, heads, group_ref, g, 0), bias_ref[...]) for g in range(groups)]
    for g in range(groups):
        weight_ref[g], inverse = softmax_parts(scores[g])
        inverse_ref[g] = jnp.broadcast_to(inverse, inverse_ref.shape[1:])


def mix_kernel(heads, group_ref, weight_ref, inverse_ref, v_ref, *refs):
    *rims, out_ref, buf, sem = refs
    groups = weight_ref.shape[0]
    if heads:
        *rims, done_ref = rims
        far = pltpu.make_async_copy(done_ref, out_ref.at[pl.ds(buf.shape[0], done_ref.shape[0])], sem.at[groups])
        far.start()
    for g in range(groups):
        value = with_rim(v_ref, rims, heads, group_ref, g, v_ref.shape[1])
        store_heads(buf, g, mix(weight_ref[g], inverse_ref[g], value))
        send_out(buf, out_ref, 0, g, sem).start()
    for g in range(groups):
        send_out(buf, out_ref, 0, g, sem).wait()
    if heads:
        far.wait()


SMEM = pl.BlockSpec(memory_space=pltpu.SMEM)
VMEM = pl.BlockSpec(memory_space=pltpu.VMEM)
ANY = pl.BlockSpec(memory_space=pl.ANY)


def cycles(devices, period):
    firsts = [0, period // 2 + 1] + [m - 1 for m in range(period, devices, period)] + [devices]
    pairs = []
    for a, b in zip(firsts, firsts[1:]):
        pairs += [(i, i + 1) for i in range(a, b - 1)] + [(b - 1, a)]
    return pairs, firsts[1:-1]


def on_device(queries, key_rows, value_rows, group_kv_head, doc_ids):
    rows, width = queries.shape
    devices = lax.axis_size("ctx") * lax.axis_size("head")
    period = 2 * lax.axis_size("head")
    groups = width // WIDTH
    reach = rows * lax.axis_size("head") // 8
    near = min(reach, rows)
    hops = -(-reach // rows)
    small = near < rows
    dtype = queries.dtype
    docs = doc_ids.reshape(devices, rows)
    if small:
        chain, heads = cycles(devices, period)
        pairs = [(i, i ^ 1) for i in range(devices)]
        sent = {}
        for name, array, moves in (("main_k", key_rows, chain), ("main_v", value_rows, chain),
                                   ("side_k", key_rows, pairs), ("side_v", value_rows, pairs)):
            sent[name] = lax.ppermute(array, AXES, moves)
        key_rims, value_rims = [sent["main_k"], sent["side_k"]], [sent["main_v"], sent["side_v"]]
    else:
        edge = jnp.concatenate([key_rows, value_rows], axis=1)
        key_rims = value_rims = [
            lax.ppermute(edge, AXES, [(i, i + j) for i in range(devices - j)]) for j in range(1, hops + 1)]
    vmem = lambda x: pltpu.with_memory_space_constraint(x, pltpu.VMEM) if small else x
    chip = pltpu.VMEM if small else jax.ShapeDtypeStruct
    keys = 2 * near if small else rows * (1 + hops)
    far = (rows - near, width)
    group, near_q, near_k, near_v, bias, *done = pl.pallas_call(
        functools.partial(inner_kernel, near, hops),
        out_shape=[
            pltpu.SMEM(group_kv_head.shape, jnp.int32), chip((near, width), dtype),
            chip((near, key_rows.shape[1]), dtype), chip((near, key_rows.shape[1]), dtype), chip((near, keys), jnp.float32),
        ] + [chip(far, dtype)] * small,
        in_specs=[ANY] * 5, out_specs=[SMEM] + [VMEM] * (4 + small), name="inner",
        scratch_shapes=[
            pltpu.SMEM(group_kv_head.shape, jnp.int32), pltpu.VMEM(docs.shape, jnp.int32),
            pltpu.VMEM(key_rows.shape, dtype), pltpu.VMEM(key_rows.shape, dtype), pltpu.SemaphoreType.DMA((6,)),
        ] + [pltpu.VMEM(far, dtype)] * small,
    )(group_kv_head, docs, queries, key_rows, value_rows)
    heads = heads if small else ()
    stack = HEADS_DEV * near
    weights, inverse = pl.pallas_call(
        functools.partial(weight_kernel, heads),
        out_shape=[chip((groups, stack, keys), dtype), chip((groups, stack, HEAD_DIM), jnp.float32)],
        in_specs=[SMEM] + [VMEM] * (3 + len(key_rims)), out_specs=[VMEM] * 2, name="weights",
    )(group, *[vmem(x) for x in (near_q, bias, near_k, *key_rims)])
    ins = [vmem(x) for x in (weights, inverse, near_v, *value_rims, *done)]
    return pl.pallas_call(
        functools.partial(mix_kernel, heads),
        out_shape=jax.ShapeDtypeStruct(queries.shape, dtype),
        in_specs=[SMEM] + [VMEM] * len(ins), out_specs=ANY, name="mix",
        scratch_shapes=[pltpu.VMEM((near, width), dtype), pltpu.SemaphoreType.DMA((groups + 1,))],
    )(group, *ins)


def solution(mesh):
    placed = P(AXES, None)
    return jax.shard_map(
        on_device, mesh=mesh, in_specs=(placed, placed, placed, P(), P()), out_specs=placed, check_vma=False
    )
```

```python
import functools
import math

import jax
import jax.numpy as jnp
from jax import lax
from jax.experimental import pallas as pl
from jax.experimental.pallas import tpu as pltpu
from jax.sharding import PartitionSpec as P


HEAD_DIM = 128
HEADS_DEV = 4
WIDTH = HEADS_DEV * HEAD_DIM
AXES = ("ctx", "head")
neg_fill = -1e30
FACTOR = math.log2(math.e) / math.sqrt(HEAD_DIM)


def flat_index():
    return lax.axis_index("ctx") * lax.axis_size("head") + lax.axis_index("head")


def bias_of(visible):
    return jnp.where(visible, 0.0, neg_fill)


def scores_of(query, key, bias):
    raw = lax.dot_general(query, key, (((1,), (1,)), ((), ())), preferred_element_type=jnp.float32)
    return raw * FACTOR + jnp.concatenate([bias] * HEADS_DEV, axis=0)


def tall_scores(query, key, bias):
    raw = lax.dot_general(key, query, (((1,), (1,)), ((), ())), preferred_element_type=jnp.float32)
    return raw * FACTOR + bias


def softmax_parts(scores):
    expo = jnp.exp2(scores - jnp.max(scores, axis=1, keepdims=True))
    inverse = 1.0 / jnp.sum(expo, axis=1, keepdims=True)
    return expo.astype(jnp.bfloat16), inverse


def mix(weights, inverse, value):
    return (jnp.dot(weights, value, preferred_element_type=jnp.float32) * inverse).astype(jnp.bfloat16)


def column_of(row):
    return jnp.transpose(jnp.broadcast_to(row, (row.shape[1], row.shape[1])))


def head_stack(ref, g):
    return jnp.concatenate(
        [ref[:, g * WIDTH + h * HEAD_DIM:g * WIDTH + (h + 1) * HEAD_DIM] for h in range(HEADS_DEV)], axis=0)


def store_heads(ref, g, result):
    n = result.shape[0] // HEADS_DEV
    for h in range(HEADS_DEV):
        ref[:, g * WIDTH + h * HEAD_DIM:g * WIDTH + (h + 1) * HEAD_DIM] = result[h * n:(h + 1) * n]


def send_out(buf, out_ref, first, g, sem):
    cols = pl.ds(g * WIDTH, WIDTH)
    return pltpu.make_async_copy(buf.at[:, cols], out_ref.at[pl.ds(first, buf.shape[0]), cols], sem.at[g])


def columns(group_ref, g, offset=0):
    return pl.ds(pl.multiple_of(group_ref[g] * HEAD_DIM + offset, HEAD_DIM), HEAD_DIM)


def load_kernel(near, group_hbm, doc_hbm, k_hbm, v_hbm, value_ref, edge_ref, group_ref, doc_ref, sem):
    last, width = pl.ds(k_hbm.shape[0] - near, near), k_hbm.shape[1]
    loads = [(v_hbm.at[last], value_ref), (k_hbm.at[last], edge_ref.at[:, pl.ds(0, width)]),
             (v_hbm.at[last], edge_ref.at[:, pl.ds(width, width)]), (doc_hbm, doc_ref), (group_hbm, group_ref)]
    loads = [pltpu.make_async_copy(a, b, sem.at[i]) for i, (a, b) in enumerate(loads)]
    for load in loads:
        load.start()
    for load in loads:
        load.wait()


def inner_kernel(hops, group_ref, doc_ref, q_hbm, k_hbm, v_hbm, bias_ref, near_q, k_ref, v_ref, *refs):
    (rows, width), near = q_hbm.shape, near_q.shape[0]
    groups = width // WIDTH
    *refs, sem = refs
    loads = [(k_hbm, k_ref), (v_hbm, v_ref), (q_hbm.at[pl.ds(0, near)], near_q)]
    if near < rows:
        out_ref, far_q = refs
        loads.insert(0, (q_hbm.at[pl.ds(near, rows - near)], far_q))
    loads = [pltpu.make_async_copy(a, b, sem.at[i]) for i, (a, b) in enumerate(loads)]
    for load in loads:
        load.start()
    me = flat_index()
    own = doc_ref[pl.ds(me, 1), :]
    before = [doc_ref[pl.ds(jnp.maximum(me - j, 0), 1), :] for j in range(1, hops + 1)]
    col = column_of(own)
    t = lax.broadcasted_iota(jnp.int32, (rows, rows), 0)
    u = lax.broadcasted_iota(jnp.int32, (rows, rows), 1)
    own_bias = bias_of((own == col) & (u <= t))
    if near == rows:
        seen = [(col == own) & (t <= u)]
        seen += [(column_of(before[j]) == own) & (t + (me - 1 - j) * rows >= 0) for j in range(hops)]
        seen = [bias_of(part) for part in seen]
    else:
        docs = column_of(jnp.where(lax.broadcasted_iota(jnp.int32, own.shape, 1) < near, own, before[0]))
        pos = jnp.where(t < near, t, t - rows)
        seen = [bias_of((docs == own) & (pos <= u) & (pos + me * rows >= 0))[:, :near]]
    bias_ref[...] = jnp.concatenate([jnp.concatenate(seen, axis=0)] * HEADS_DEV, axis=1)
    for load in loads[:-1]:
        load.wait()
    if near < rows:
        for g in range(groups):
            c = columns(group_ref, g)
            scores = scores_of(head_stack(far_q, g), k_ref[:, c], own_bias[near:])
            store_heads(out_ref, g, mix(*softmax_parts(scores), v_ref[:, c]))
    loads[-1].wait()


def with_rim(own_ref, near, rims, heads, group_ref, g, offset):
    here = columns(group_ref, g)
    if heads:
        me = flat_index()
        swap = functools.reduce(jnp.logical_or, [me == head for head in heads])
        main, side = rims
        parts = [jnp.where(swap, side[:, columns(group_ref, g, offset)], main[main.shape[0] - near:, here])]
    else:
        parts = [r[:, columns(group_ref, g, offset)] for r in rims]
    return jnp.concatenate([own_ref[:near, here]] + parts, axis=0)


def weight_kernel(heads, group_ref, q_ref, bias_ref, k_ref, *refs):
    *rims, weight_ref, inverse_ref = refs
    groups, near = q_ref.shape[1] // WIDTH, q_ref.shape[0]
    scores = [
        tall_scores(head_stack(q_ref, g), with_rim(k_ref, near, rims, heads, group_ref, g, 0), bias_ref[...])
        for g in range(groups)]
    totals = []
    for g in range(groups):
        expo = jnp.exp2(scores[g] - jnp.max(scores[g], axis=0, keepdims=True))
        weight_ref[g] = jnp.transpose(expo.astype(jnp.bfloat16))
        totals.append(jnp.sum(expo, axis=0, keepdims=True))
    spare = inverse_ref.shape[1] - groups
    inverse = 1.0 / jnp.concatenate(totals, axis=0)
    inverse = jnp.concatenate([inverse, jnp.zeros((spare, inverse.shape[1]), jnp.float32)], axis=0) if spare else inverse
    inverse_ref[...] = jnp.transpose(inverse)


def mix_kernel(heads, group_ref, weight_ref, inverse_ref, v_ref, *refs):
    *rims, out_ref, buf, sem = refs
    groups = weight_ref.shape[0]
    if heads:
        *rims, done_ref = rims
        far = pltpu.make_async_copy(done_ref, out_ref.at[pl.ds(buf.shape[0], done_ref.shape[0])], sem.at[groups])
        far.start()
    for g in range(groups):
        value = with_rim(v_ref, buf.shape[0], rims, heads, group_ref, g, v_ref.shape[1])
        store_heads(buf, g, mix(weight_ref[g], inverse_ref[:, g:g + 1], value))
        send_out(buf, out_ref, 0, g, sem).start()
    for g in range(groups):
        send_out(buf, out_ref, 0, g, sem).wait()
    if heads:
        far.wait()


SMEM = pl.BlockSpec(memory_space=pltpu.SMEM)
VMEM = pl.BlockSpec(memory_space=pltpu.VMEM)
ANY = pl.BlockSpec(memory_space=pl.ANY)


def cycles(devices, period):
    firsts = [0, period // 2 + 1] + [m - 1 for m in range(period, devices, period)] + [devices]
    pairs = []
    for a, b in zip(firsts, firsts[1:]):
        pairs += [(i, i + 1) for i in range(a, b - 1)] + [(b - 1, a)]
    return pairs, firsts[1:-1]


def on_device(queries, key_rows, value_rows, group_kv_head, doc_ids):
    rows, width = queries.shape
    devices = lax.axis_size("ctx") * lax.axis_size("head")
    period = 2 * lax.axis_size("head")
    groups = width // WIDTH
    reach = rows * lax.axis_size("head") // 8
    near = min(reach, rows)
    hops = -(-reach // rows)
    small = near < rows
    dtype = queries.dtype
    docs = doc_ids.reshape(devices, rows)
    vmem = lambda x: pltpu.with_memory_space_constraint(x, pltpu.VMEM) if small else x
    chip = pltpu.VMEM if small else jax.ShapeDtypeStruct
    keys = 2 * near if small else rows * (1 + hops)
    kv_shape = key_rows.shape
    value_edge, edge, group, near_docs = pl.pallas_call(
        functools.partial(load_kernel, near),
        out_shape=[
            chip((near, kv_shape[1]), dtype), chip((near, 2 * kv_shape[1]), dtype),
            pltpu.SMEM(group_kv_head.shape, jnp.int32), chip(docs.shape, jnp.int32),
        ],
        in_specs=[ANY] * 4, out_specs=[VMEM] * 2 + [SMEM, VMEM], name="load",
        scratch_shapes=[pltpu.SemaphoreType.DMA((5,))],
    )(group_kv_head, docs, key_rows, value_rows)
    bias, q, k, v, *done = pl.pallas_call(
        functools.partial(inner_kernel, hops),
        out_shape=[chip((keys, HEADS_DEV * near), jnp.float32), chip((near, width), dtype), chip(kv_shape, dtype), chip(kv_shape, dtype)]
        + [chip((rows - near, width), dtype)] * small,
        in_specs=[SMEM, VMEM] + [ANY] * 3, out_specs=[VMEM] * (4 + small), name="inner",
        scratch_shapes=[pltpu.VMEM((rows - near, width), dtype)] * small + [pltpu.SemaphoreType.DMA((4,))],
    )(group, vmem(near_docs), queries, key_rows, value_rows)
    if small:
        chain, heads = cycles(devices, period)
        pairs = [(i, i ^ 1) for i in range(devices)]
        sent = {}
        for name, array, moves in (("main_k", key_rows, chain), ("main_v", value_edge, chain), ("side", edge, pairs)):
            sent[name] = lax.ppermute(array, AXES, moves)
        key_rims, value_rims = [sent["main_k"], sent["side"]], [sent["main_v"], sent["side"]]
    else:
        key_rims = value_rims = [
            lax.ppermute(edge, AXES, [(i, i + j) for i in range(devices - j)]) for j in range(1, hops + 1)]
    heads = heads if small else ()
    stack = HEADS_DEV * near
    weights, inverse = pl.pallas_call(
        functools.partial(weight_kernel, heads),
        out_shape=[chip((groups, stack, keys), dtype), chip((stack, -(-groups // 8) * 8), jnp.float32)],
        in_specs=[SMEM] + [VMEM] * (3 + len(key_rims)), out_specs=[VMEM] * 2, name="weights",
    )(group, *[vmem(x) for x in (q, bias, k, *key_rims)])
    ins = [vmem(x) for x in (weights, inverse, v, *value_rims, *done)]
    return pl.pallas_call(
        functools.partial(mix_kernel, heads),
        out_shape=jax.ShapeDtypeStruct(queries.shape, dtype),
        in_specs=[SMEM] + [VMEM] * len(ins), out_specs=ANY, name="mix",
        scratch_shapes=[pltpu.VMEM((near, width), dtype), pltpu.SemaphoreType.DMA((groups + 1,))],
    )(group, *ins)


def solution(mesh):
    placed = P(AXES, None)
    return jax.shard_map(
        on_device, mesh=mesh, in_specs=(placed, placed, placed, P(), P()), out_specs=placed, check_vma=False
    )
```

```python
import functools
import math

import jax
import jax.numpy as jnp
from jax import lax
from jax.experimental import pallas as pl
from jax.experimental.pallas import tpu as pltpu
from jax.sharding import PartitionSpec as P


HEAD_DIM = 128
HEADS_DEV = 4
WIDTH = HEADS_DEV * HEAD_DIM
AXES = ("ctx", "head")
neg_fill = -1e30
FACTOR = math.log2(math.e) / math.sqrt(HEAD_DIM)


def flat_index():
    return lax.axis_index("ctx") * lax.axis_size("head") + lax.axis_index("head")


def bias_of(visible):
    return jnp.where(visible, 0.0, neg_fill)


def scores_of(query, key, bias):
    raw = lax.dot_general(query, key, (((1,), (1,)), ((), ())), preferred_element_type=jnp.float32)
    return raw * FACTOR + jnp.concatenate([bias] * HEADS_DEV, axis=0)


def tall_scores(query, key, bias):
    raw = lax.dot_general(key, query, (((1,), (1,)), ((), ())), preferred_element_type=jnp.float32)
    return raw * FACTOR + bias


def softmax_parts(scores):
    expo = jnp.exp2(scores - jnp.max(scores, axis=1, keepdims=True))
    inverse = 1.0 / jnp.sum(expo, axis=1, keepdims=True)
    return expo.astype(jnp.bfloat16), inverse


def mix(weights, inverse, value):
    return (jnp.dot(weights, value, preferred_element_type=jnp.float32) * inverse).astype(jnp.bfloat16)


def column_of(row):
    return jnp.transpose(jnp.broadcast_to(row, (row.shape[1], row.shape[1])))


def head_stack(ref, g):
    return jnp.concatenate(
        [ref[:, g * WIDTH + h * HEAD_DIM:g * WIDTH + (h + 1) * HEAD_DIM] for h in range(HEADS_DEV)], axis=0)


def store_heads(ref, g, result):
    n = result.shape[0] // HEADS_DEV
    for h in range(HEADS_DEV):
        ref[:, g * WIDTH + h * HEAD_DIM:g * WIDTH + (h + 1) * HEAD_DIM] = result[h * n:(h + 1) * n]


def send_out(buf, out_ref, first, g, sem):
    cols = pl.ds(g * WIDTH, WIDTH)
    return pltpu.make_async_copy(buf.at[:, cols], out_ref.at[pl.ds(first, buf.shape[0]), cols], sem.at[g])


def columns(group_ref, g, offset=0):
    late, early = group_ref
    return pl.ds(pl.multiple_of(jnp.where(first_pair(), early[g], late[g]) * HEAD_DIM + offset, HEAD_DIM), HEAD_DIM)


def run_all(pairs, sem):
    copies = [pltpu.make_async_copy(a, b, sem.at[i]) for i, (a, b) in enumerate(pairs)]
    for copy in copies:
        copy.start()
    for copy in copies:
        copy.wait()


def first_pair():
    return flat_index() < 2


def last_rows(hbm, near):
    return hbm.at[pl.ds(hbm.shape[0] - near, near)]


def own_loads(doc_hbm, q_hbm, k_hbm, v_hbm, edge_ref, doc_ref, q_ref, k_ref, v_ref):
    near, width = edge_ref.shape[0], k_hbm.shape[1]
    return [(last_rows(k_hbm, near), edge_ref.at[:, pl.ds(0, width)]), (last_rows(v_hbm, near), edge_ref.at[:, pl.ds(width, width)]),
            (doc_hbm, doc_ref), (k_hbm, k_ref), (v_hbm, v_ref), (q_hbm, q_ref)]


def edge_kernel(group_hbm, doc_hbm, q_hbm, k_hbm, v_hbm, key_ref, value_ref, group_ref, *refs):
    *refs, sem = refs
    near = key_ref.shape[0]
    pairs = [(last_rows(k_hbm, near), key_ref), (last_rows(v_hbm, near), value_ref)]

    me = flat_index()

    @pl.when((me % 2 == 1) | (me == 0))
    def _():
        copies = [pltpu.make_async_copy(a, b, sem.at[i]) for i, (a, b) in enumerate(pairs)]
        for copy in copies:
            copy.start()

        @pl.when(first_pair())
        def _():
            run_all([(group_hbm, group_ref)] + own_loads(doc_hbm, q_hbm, k_hbm, v_hbm, *refs), sem.at[pl.ds(len(pairs), 7)])

        for copy in copies:
            copy.wait()


def load_kernel(given, group_hbm, doc_hbm, q_hbm, k_hbm, v_hbm, *refs):
    group_ref, *refs, sem = refs[given:]
    loads = [(group_hbm, group_ref)] + own_loads(doc_hbm, q_hbm, k_hbm, v_hbm, *refs)
    if not given:
        run_all(loads, sem)
        return

    @pl.when(jnp.logical_not(first_pair()))
    def _():
        run_all(loads, sem)


def inner_kernel(near, hops, group_ref, other_ref, doc_ref, q_ref, k_ref, v_ref, bias_ref, *out_ref):
    rows, width = q_ref.shape
    me = flat_index()
    own = doc_ref[pl.ds(me, 1), :]
    before = [doc_ref[pl.ds(jnp.maximum(me - j, 0), 1), :] for j in range(1, hops + 1)]
    col = column_of(own)
    t = lax.broadcasted_iota(jnp.int32, (rows, rows), 0)
    u = lax.broadcasted_iota(jnp.int32, (rows, rows), 1)
    if near == rows:
        seen = [(col == own) & (t <= u)]
        seen += [(column_of(before[j]) == own) & (t + (me - 1 - j) * rows >= 0) for j in range(hops)]
        seen = [bias_of(part) for part in seen]
    else:
        docs = column_of(jnp.where(lax.broadcasted_iota(jnp.int32, own.shape, 1) < near, own, before[0]))
        pos = jnp.where(t < near, t, t - rows)
        seen = [bias_of((docs == own) & (pos <= u) & (pos + me * rows >= 0))[:, :near]]
    bias_ref[...] = jnp.concatenate([jnp.concatenate(seen, axis=0)] * HEADS_DEV, axis=1)
    if near < rows:
        bias = bias_of((own == col) & (u <= t))[near:]
        far = q_ref.at[pl.ds(near, rows - near)]
        for g in range(width // WIDTH):
            c = columns((group_ref, other_ref), g)
            scores = scores_of(head_stack(far, g), k_ref[:, c], bias)
            store_heads(out_ref[0], g, mix(*softmax_parts(scores), v_ref[:, c]))


def with_rim(own_ref, near, rims, small, group_ref, g, offset):
    here = columns(group_ref, g)
    if small:
        me = flat_index()
        main, side = rims
        parts = [jnp.where((me % 2 == 1) | (me == 0), side[:, columns(group_ref, g, offset)], main[:, here])]
    else:
        parts = [r[:, columns(group_ref, g, offset)] for r in rims]
    return jnp.concatenate([own_ref[:near, here]] + parts, axis=0)


def weight_kernel(small, group_ref, other_ref, q_ref, bias_ref, k_ref, *refs):
    *rims, weight_ref, inverse_ref = refs
    groups, near = q_ref.shape[1] // WIDTH, weight_ref.shape[1] // HEADS_DEV
    q_ref = q_ref.at[pl.ds(0, near)]
    scores = [
        tall_scores(head_stack(q_ref, g), with_rim(k_ref, near, rims, small, (group_ref, other_ref), g, 0), bias_ref[...])
        for g in range(groups)]
    totals = []
    for g in range(groups):
        expo = jnp.exp2(scores[g] - jnp.max(scores[g], axis=0, keepdims=True))
        weight_ref[g] = jnp.transpose(expo.astype(jnp.bfloat16))
        totals.append(jnp.sum(expo, axis=0, keepdims=True))
    spare = inverse_ref.shape[1] - groups
    inverse = 1.0 / jnp.concatenate(totals, axis=0)
    inverse = jnp.concatenate([inverse, jnp.zeros((spare, inverse.shape[1]), jnp.float32)], axis=0) if spare else inverse
    inverse_ref[...] = jnp.transpose(inverse)


def mix_kernel(small, group_ref, other_ref, weight_ref, inverse_ref, v_ref, *refs):
    *rims, out_ref, buf, sem = refs
    groups = weight_ref.shape[0]
    if small:
        *rims, done_ref = rims
        far = pltpu.make_async_copy(done_ref, out_ref.at[pl.ds(buf.shape[0], done_ref.shape[0])], sem.at[groups])
        far.start()
    for g in range(groups):
        value = with_rim(v_ref, buf.shape[0], rims, small, (group_ref, other_ref), g, v_ref.shape[1])
        store_heads(buf, g, mix(weight_ref[g], inverse_ref[:, g:g + 1], value))
        send_out(buf, out_ref, 0, g, sem).start()
    for g in range(groups):
        send_out(buf, out_ref, 0, g, sem).wait()
    if small:
        far.wait()


SMEM = pl.BlockSpec(memory_space=pltpu.SMEM)
VMEM = pl.BlockSpec(memory_space=pltpu.VMEM)
ANY = pl.BlockSpec(memory_space=pl.ANY)


def cycles(devices, period):
    firsts = [0, period // 2 + 1] + [m - 1 for m in range(period, devices, period)] + [devices]
    pairs = []
    for a, b in zip(firsts, firsts[1:]):
        pairs += [(i, i + 1) for i in range(a, b - 1)] + [(b - 1, a)]
    return pairs


def on_device(queries, key_rows, value_rows, group_kv_head, doc_ids):
    rows, width = queries.shape
    devices = lax.axis_size("ctx") * lax.axis_size("head")
    period = 2 * lax.axis_size("head")
    groups = width // WIDTH
    reach = rows * lax.axis_size("head") // 8
    near = min(reach, rows)
    hops = -(-reach // rows)
    small = near < rows
    dtype = queries.dtype
    docs = doc_ids.reshape(devices, rows)
    vmem = lambda x: pltpu.with_memory_space_constraint(x, pltpu.VMEM) if small else x
    chip = pltpu.VMEM if small else jax.ShapeDtypeStruct
    keys = 2 * near if small else rows * (1 + hops)
    kv_shape = key_rows.shape
    sent, early, arguments = {}, [], (group_kv_head, docs, queries, key_rows, value_rows)
    tables = [chip((near, 2 * kv_shape[1]), dtype), chip(docs.shape, jnp.int32), chip(queries.shape, dtype), chip(kv_shape, dtype),
              chip(kv_shape, dtype)]
    names = pltpu.SMEM(group_kv_head.shape, jnp.int32)
    if small:
        key_edge, value_edge, early_group, *early = pl.pallas_call(
            edge_kernel, out_shape=[chip((near, kv_shape[1]), dtype)] * 2 + [names] + tables,
            in_specs=[ANY] * 5, out_specs=[VMEM] * 2 + [SMEM] + [VMEM] * 5, name="edges",
            scratch_shapes=[pltpu.SemaphoreType.DMA((9,))],
        )(*arguments)
        for name, array in (("main_k", key_edge), ("main_v", value_edge)):
            sent[name] = lax.ppermute(array, AXES, cycles(devices, period))
    group, edge, near_docs, q, k, v = pl.pallas_call(
        functools.partial(load_kernel, len(early)), out_shape=[names] + tables,
        in_specs=[ANY] * 5 + [VMEM] * len(early), out_specs=[SMEM] + [VMEM] * 5, name="load",
        scratch_shapes=[pltpu.SemaphoreType.DMA((7,))],
        input_output_aliases={5 + i: 1 + i for i in range(len(early))},
    )(*arguments, *[vmem(x) for x in early])
    groups_of = (group, early_group if small else group)
    bias, *done = pl.pallas_call(
        functools.partial(inner_kernel, near, hops),
        out_shape=[chip((keys, HEADS_DEV * near), jnp.float32)] + [chip((rows - near, width), dtype)] * small,
        in_specs=[SMEM] * 2 + [VMEM] * 4, out_specs=[VMEM] * (1 + small), name="inner",
    )(*groups_of, *[vmem(x) for x in (near_docs, q, k, v)])
    if small:
        side = lax.ppermute(edge, AXES, [(i, i ^ 1) for i in range(devices)])
        key_rims, value_rims = [sent["main_k"], side], [sent["main_v"], side]
    else:
        key_rims = value_rims = [
            lax.ppermute(edge, AXES, [(i, i + j) for i in range(devices - j)]) for j in range(1, hops + 1)]
    stack = HEADS_DEV * near
    weights, inverse = pl.pallas_call(
        functools.partial(weight_kernel, small),
        out_shape=[chip((groups, stack, keys), dtype), chip((stack, -(-groups // 8) * 8), jnp.float32)],
        in_specs=[SMEM] * 2 + [VMEM] * (3 + len(key_rims)), out_specs=[VMEM] * 2, name="weights",
    )(*groups_of, *[vmem(x) for x in (q, bias, k, *key_rims)])
    ins = [vmem(x) for x in (weights, inverse, v, *value_rims, *done)]
    return pl.pallas_call(
        functools.partial(mix_kernel, small),
        out_shape=jax.ShapeDtypeStruct(queries.shape, dtype),
        in_specs=[SMEM] * 2 + [VMEM] * len(ins), out_specs=ANY, name="mix",
        scratch_shapes=[pltpu.VMEM((near, width), dtype), pltpu.SemaphoreType.DMA((groups + 1,))],
    )(*groups_of, *ins)


def solution(mesh):
    placed = P(AXES, None)
    return jax.shard_map(
        on_device, mesh=mesh, in_specs=(placed, placed, placed, P(), P()), out_specs=placed, check_vma=False
    )
```

```python
import functools
import math

import jax
import jax.numpy as jnp
from jax import lax
from jax.experimental import pallas as pl
from jax.experimental.pallas import tpu as pltpu
from jax.sharding import PartitionSpec as P


HEAD_DIM = 128
HEADS_DEV = 4
WIDTH = HEADS_DEV * HEAD_DIM
AXES = ("ctx", "head")
neg_fill = -1e30
FACTOR = math.log2(math.e) / math.sqrt(HEAD_DIM)


def flat_index():
    return lax.axis_index("ctx") * lax.axis_size("head") + lax.axis_index("head")


def bias_of(visible):
    return jnp.where(visible, 0.0, neg_fill)


def scores_of(query, key, bias):
    raw = lax.dot_general(query, key, (((1,), (1,)), ((), ())), preferred_element_type=jnp.float32)
    return raw * FACTOR + jnp.concatenate([bias] * HEADS_DEV, axis=0)


def tall_scores(query, key, bias):
    raw = lax.dot_general(key, query, (((1,), (1,)), ((), ())), preferred_element_type=jnp.float32)
    return raw * FACTOR + bias


def softmax_parts(scores):
    expo = jnp.exp2(scores - jnp.max(scores, axis=1, keepdims=True))
    inverse = 1.0 / jnp.sum(expo, axis=1, keepdims=True)
    return expo.astype(jnp.bfloat16), inverse


def mix(weights, inverse, value):
    return (jnp.dot(weights, value, preferred_element_type=jnp.float32) * inverse).astype(jnp.bfloat16)


def column_of(row):
    return jnp.transpose(jnp.broadcast_to(row, (row.shape[1], row.shape[1])))


def head_stack(ref, g):
    return jnp.concatenate(
        [ref[:, g * WIDTH + h * HEAD_DIM:g * WIDTH + (h + 1) * HEAD_DIM] for h in range(HEADS_DEV)], axis=0)


def store_heads(ref, g, result):
    n = result.shape[0] // HEADS_DEV
    for h in range(HEADS_DEV):
        ref[:, g * WIDTH + h * HEAD_DIM:g * WIDTH + (h + 1) * HEAD_DIM] = result[h * n:(h + 1) * n]


def send_out(buf, out_ref, first, g, sem):
    cols = pl.ds(g * WIDTH, WIDTH)
    return pltpu.make_async_copy(buf.at[:, cols], out_ref.at[pl.ds(first, buf.shape[0]), cols], sem.at[g])


def columns(group_ref, g, offset=0):
    late, early = group_ref
    return pl.ds(pl.multiple_of(jnp.where(first_pair(), early[g], late[g]) * HEAD_DIM + offset, HEAD_DIM), HEAD_DIM)


def run_all(pairs, sem):
    copies = [pltpu.make_async_copy(a, b, sem.at[i]) for i, (a, b) in enumerate(pairs)]
    for copy in copies:
        copy.start()
    for copy in copies:
        copy.wait()


def first_pair():
    return flat_index() < 2


def last_rows(hbm, near):
    return hbm.at[pl.ds(hbm.shape[0] - near, near)]


def edge_loads(k_hbm, v_hbm, edge_ref):
    near, width = edge_ref.shape[0], k_hbm.shape[1]
    return [(last_rows(k_hbm, near), edge_ref.at[:, pl.ds(0, width)]), (last_rows(v_hbm, near), edge_ref.at[:, pl.ds(width, width)])]


def own_loads(doc_hbm, q_hbm, k_hbm, v_hbm, doc_ref, q_ref, k_ref, v_ref):
    return [(doc_hbm, doc_ref), (k_hbm, k_ref), (v_hbm, v_ref), (q_hbm, q_ref)]


def edge_kernel(group_hbm, doc_hbm, q_hbm, k_hbm, v_hbm, key_ref, value_ref, group_ref, *refs):
    *refs, sem = refs
    extra = (key_ref.shape[0] - value_ref.shape[0]) // 2
    near, rest = key_ref.shape[0] - extra, value_ref.shape[0]
    pairs = [(last_rows(k_hbm, near), key_ref.at[pl.ds(0, near)]), (last_rows(v_hbm, rest), value_ref),
             (v_hbm.at[pl.ds(v_hbm.shape[0] - near, extra)], key_ref.at[pl.ds(near, extra)])]

    me = flat_index()

    @pl.when((me % 2 == 1) | (me == 0))
    def _():
        copies = [pltpu.make_async_copy(a, b, sem.at[i]) for i, (a, b) in enumerate(pairs)]
        for copy in copies:
            copy.start()

        @pl.when(first_pair())
        def _():
            run_all([(group_hbm, group_ref)] + own_loads(doc_hbm, q_hbm, k_hbm, v_hbm, *refs), sem.at[pl.ds(len(pairs), 5)])

        for copy in copies:
            copy.wait()


def load_kernel(given, group_hbm, doc_hbm, q_hbm, k_hbm, v_hbm, *refs):
    edge_ref, group_ref, *refs, sem = refs[given:]
    loads = [(group_hbm, group_ref)] + own_loads(doc_hbm, q_hbm, k_hbm, v_hbm, *refs)
    if not given:
        run_all(edge_loads(k_hbm, v_hbm, edge_ref) + loads, sem)
        return

    @pl.when(first_pair())
    def _():
        edge_ref[:, :k_hbm.shape[1]] = refs[2][refs[2].shape[0] - edge_ref.shape[0]:]
        edge_ref[:, k_hbm.shape[1]:] = refs[3][refs[3].shape[0] - edge_ref.shape[0]:]

    @pl.when(jnp.logical_not(first_pair()))
    def _():
        run_all(edge_loads(k_hbm, v_hbm, edge_ref) + loads, sem)


def inner_kernel(near, hops, group_ref, other_ref, doc_ref, q_ref, k_ref, v_ref, bias_ref, *out_ref):
    rows, width = q_ref.shape
    me = flat_index()
    own = doc_ref[pl.ds(me, 1), :]
    before = [doc_ref[pl.ds(jnp.maximum(me - j, 0), 1), :] for j in range(1, hops + 1)]
    col = column_of(own)
    t = lax.broadcasted_iota(jnp.int32, (rows, rows), 0)
    u = lax.broadcasted_iota(jnp.int32, (rows, rows), 1)
    if near == rows:
        seen = [(col == own) & (t <= u)]
        seen += [(column_of(before[j]) == own) & (t + (me - 1 - j) * rows >= 0) for j in range(hops)]
        seen = [bias_of(part) for part in seen]
    else:
        docs = column_of(jnp.where(lax.broadcasted_iota(jnp.int32, own.shape, 1) < near, own, before[0]))
        pos = jnp.where(t < near, t, t - rows)
        seen = [bias_of((docs == own) & (pos <= u) & (pos + me * rows >= 0))[:, :near]]
    bias_ref[...] = jnp.concatenate([jnp.concatenate(seen, axis=0)] * HEADS_DEV, axis=1)
    if near < rows:
        bias = bias_of((own == col) & (u <= t))[near:]
        far = q_ref.at[pl.ds(near, rows - near)]
        for g in range(width // WIDTH):
            c = columns((group_ref, other_ref), g)
            scores = scores_of(head_stack(far, g), k_ref[:, c], bias)
            store_heads(out_ref[0], g, mix(*softmax_parts(scores), v_ref[:, c]))


def with_rim(own_ref, near, rims, small, group_ref, g, offset):
    here = columns(group_ref, g)
    if small:
        me = flat_index()
        *main, side = rims
        if offset:
            main = jnp.concatenate([main[0][near:, here], main[1][:, here]], axis=0)
        else:
            main = main[0][:near, here]
        parts = [jnp.where((me % 2 == 1) | (me == 0), side[:, columns(group_ref, g, offset)], main)]
    else:
        parts = [r[:, columns(group_ref, g, offset)] for r in rims]
    return jnp.concatenate([own_ref[:near, here]] + parts, axis=0)


def weight_kernel(small, group_ref, other_ref, q_ref, bias_ref, k_ref, *refs):
    *rims, weight_ref, inverse_ref = refs
    groups, near = q_ref.shape[1] // WIDTH, weight_ref.shape[1] // HEADS_DEV
    q_ref = q_ref.at[pl.ds(0, near)]
    scores = [
        tall_scores(head_stack(q_ref, g), with_rim(k_ref, near, rims, small, (group_ref, other_ref), g, 0), bias_ref[...])
        for g in range(groups)]
    totals = []
    for g in range(groups):
        expo = jnp.exp2(scores[g] - jnp.max(scores[g], axis=0, keepdims=True))
        weight_ref[g] = jnp.transpose(expo.astype(jnp.bfloat16))
        totals.append(jnp.sum(expo, axis=0, keepdims=True))
    spare = inverse_ref.shape[1] - groups
    inverse = 1.0 / jnp.concatenate(totals, axis=0)
    inverse = jnp.concatenate([inverse, jnp.zeros((spare, inverse.shape[1]), jnp.float32)], axis=0) if spare else inverse
    inverse_ref[...] = jnp.transpose(inverse)


def mix_kernel(small, group_ref, other_ref, weight_ref, inverse_ref, v_ref, *refs):
    *rims, out_ref, buf, sem = refs
    groups = weight_ref.shape[0]
    if small:
        *rims, done_ref = rims
        far = pltpu.make_async_copy(done_ref, out_ref.at[pl.ds(buf.shape[0], done_ref.shape[0])], sem.at[groups])
        far.start()
    for g in range(groups):
        value = with_rim(v_ref, buf.shape[0], rims, small, (group_ref, other_ref), g, v_ref.shape[1])
        store_heads(buf, g, mix(weight_ref[g], inverse_ref[:, g:g + 1], value))
        send_out(buf, out_ref, 0, g, sem).start()
    for g in range(groups):
        send_out(buf, out_ref, 0, g, sem).wait()
    if small:
        far.wait()


SMEM = pl.BlockSpec(memory_space=pltpu.SMEM)
VMEM = pl.BlockSpec(memory_space=pltpu.VMEM)
ANY = pl.BlockSpec(memory_space=pl.ANY)


def cycles(devices, period):
    firsts = [0, period // 2 + 1] + [m - 1 for m in range(period, devices, period)] + [devices]
    pairs = []
    for a, b in zip(firsts, firsts[1:]):
        pairs += [(i, i + 1) for i in range(a, b - 1)] + [(b - 1, a)]
    return pairs


def on_device(queries, key_rows, value_rows, group_kv_head, doc_ids):
    rows, width = queries.shape
    devices = lax.axis_size("ctx") * lax.axis_size("head")
    period = 2 * lax.axis_size("head")
    groups = width // WIDTH
    reach = rows * lax.axis_size("head") // 8
    near = min(reach, rows)
    hops = -(-reach // rows)
    small = near < rows
    dtype = queries.dtype
    docs = doc_ids.reshape(devices, rows)
    vmem = lambda x: pltpu.with_memory_space_constraint(x, pltpu.VMEM) if small else x
    chip = pltpu.VMEM if small else jax.ShapeDtypeStruct
    keys = 2 * near if small else rows * (1 + hops)
    kv_shape = key_rows.shape
    sent, early, arguments = {}, [], (group_kv_head, docs, queries, key_rows, value_rows)
    tables = [chip(docs.shape, jnp.int32), chip(queries.shape, dtype), chip(kv_shape, dtype), chip(kv_shape, dtype)]
    names = pltpu.SMEM(group_kv_head.shape, jnp.int32)
    if small:
        extra = near // 4
        key_edge, value_edge, early_group, *early = pl.pallas_call(
            edge_kernel,
            out_shape=[chip((near + extra, kv_shape[1]), dtype), chip((near - extra, kv_shape[1]), dtype), names] + tables,
            in_specs=[ANY] * 5, out_specs=[VMEM] * 2 + [SMEM] + [VMEM] * 4, name="edges",
            scratch_shapes=[pltpu.SemaphoreType.DMA((8,))],
        )(*arguments)
        for name, array in (("main_k", key_edge), ("main_v", value_edge)):
            sent[name] = lax.ppermute(array, AXES, cycles(devices, period))
    edge, group, near_docs, q, k, v = pl.pallas_call(
        functools.partial(load_kernel, len(early)), out_shape=[chip((near, 2 * kv_shape[1]), dtype), names] + tables,
        in_specs=[ANY] * 5 + [VMEM] * len(early), out_specs=[VMEM, SMEM] + [VMEM] * 4, name="load",
        scratch_shapes=[pltpu.SemaphoreType.DMA((7,))],
        input_output_aliases={5 + i: 2 + i for i in range(len(early))},
    )(*arguments, *[vmem(x) for x in early])
    groups_of = (group, early_group if small else group)
    bias, *done = pl.pallas_call(
        functools.partial(inner_kernel, near, hops),
        out_shape=[chip((keys, HEADS_DEV * near), jnp.float32)] + [chip((rows - near, width), dtype)] * small,
        in_specs=[SMEM] * 2 + [VMEM] * 4, out_specs=[VMEM] * (1 + small), name="inner",
    )(*groups_of, *[vmem(x) for x in (near_docs, q, k, v)])
    if small:
        side = lax.ppermute(edge, AXES, [(i, i ^ 1) for i in range(devices)])
        key_rims, value_rims = [sent["main_k"], side], [sent["main_k"], sent["main_v"], side]
    else:
        key_rims = value_rims = [
            lax.ppermute(edge, AXES, [(i, i + j) for i in range(devices - j)]) for j in range(1, hops + 1)]
    stack = HEADS_DEV * near
    weights, inverse = pl.pallas_call(
        functools.partial(weight_kernel, small),
        out_shape=[chip((groups, stack, keys), dtype), chip((stack, -(-groups // 8) * 8), jnp.float32)],
        in_specs=[SMEM] * 2 + [VMEM] * (3 + len(key_rims)), out_specs=[VMEM] * 2, name="weights",
    )(*groups_of, *[vmem(x) for x in (q, bias, k, *key_rims)])
    ins = [vmem(x) for x in (weights, inverse, v, *value_rims, *done)]
    return pl.pallas_call(
        functools.partial(mix_kernel, small),
        out_shape=jax.ShapeDtypeStruct(queries.shape, dtype),
        in_specs=[SMEM] * 2 + [VMEM] * len(ins), out_specs=ANY, name="mix",
        scratch_shapes=[pltpu.VMEM((near, width), dtype), pltpu.SemaphoreType.DMA((groups + 1,))],
    )(*groups_of, *ins)


def solution(mesh):
    placed = P(AXES, None)
    return jax.shard_map(
        on_device, mesh=mesh, in_specs=(placed, placed, placed, P(), P()), out_specs=placed, check_vma=False
    )
```

```python
import functools
import math

import jax
import jax.numpy as jnp
from jax import lax
from jax.experimental import pallas as pl
from jax.experimental.pallas import tpu as pltpu
from jax.sharding import PartitionSpec as P


HEAD_DIM = 128
HEADS_DEV = 4
WIDTH = HEADS_DEV * HEAD_DIM
AXES = ("ctx", "head")
neg_fill = -1e30
FACTOR = math.log2(math.e) / math.sqrt(HEAD_DIM)


def flat_index():
    return lax.axis_index("ctx") * lax.axis_size("head") + lax.axis_index("head")


def bias_of(visible):
    return jnp.where(visible, 0.0, neg_fill)


def scores_of(query, key, bias):
    raw = lax.dot_general(query, key, (((1,), (1,)), ((), ())), preferred_element_type=jnp.float32)
    return raw * FACTOR + jnp.concatenate([bias] * HEADS_DEV, axis=0)


def tall_scores(query, key, bias):
    raw = lax.dot_general(key, query, (((1,), (1,)), ((), ())), preferred_element_type=jnp.float32)
    return raw * FACTOR + bias


def softmax_parts(scores):
    expo = jnp.exp2(scores - jnp.max(scores, axis=1, keepdims=True))
    inverse = 1.0 / jnp.sum(expo, axis=1, keepdims=True)
    return expo.astype(jnp.bfloat16), inverse


def mix(weights, inverse, value):
    return (jnp.dot(weights, value, preferred_element_type=jnp.float32) * inverse).astype(jnp.bfloat16)


def column_of(row):
    return jnp.transpose(jnp.broadcast_to(row, (row.shape[1], row.shape[1])))


def head_stack(ref, g):
    return jnp.concatenate(
        [ref[:, g * WIDTH + h * HEAD_DIM:g * WIDTH + (h + 1) * HEAD_DIM] for h in range(HEADS_DEV)], axis=0)


def store_heads(ref, g, result):
    n = result.shape[0] // HEADS_DEV
    for h in range(HEADS_DEV):
        ref[:, g * WIDTH + h * HEAD_DIM:g * WIDTH + (h + 1) * HEAD_DIM] = result[h * n:(h + 1) * n]


def send_out(buf, out_ref, first, g, sem):
    cols = pl.ds(g * WIDTH, WIDTH)
    return pltpu.make_async_copy(buf.at[:, cols], out_ref.at[pl.ds(first, buf.shape[0]), cols], sem.at[g])


def columns(group_ref, g, offset=0):
    late, early = group_ref
    return pl.ds(pl.multiple_of(jnp.where(first_pair(), early[g], late[g]) * HEAD_DIM + offset, HEAD_DIM), HEAD_DIM)


def run_all(pairs, sem):
    copies = [pltpu.make_async_copy(a, b, sem.at[i]) for i, (a, b) in enumerate(pairs)]
    for copy in copies:
        copy.start()
    for copy in copies:
        copy.wait()


def first_pair():
    return flat_index() < 2


def last_rows(hbm, near):
    return hbm.at[pl.ds(hbm.shape[0] - near, near)]


def edge_loads(k_hbm, v_hbm, edge_ref):
    near, width = edge_ref.shape[0], k_hbm.shape[1]
    return [(last_rows(k_hbm, near), edge_ref.at[:, pl.ds(0, width)]), (last_rows(v_hbm, near), edge_ref.at[:, pl.ds(width, width)])]


def own_loads(doc_hbm, q_hbm, k_hbm, v_hbm, doc_ref, q_ref, k_ref, v_ref):
    return [(doc_hbm, doc_ref), (k_hbm, k_ref), (v_hbm, v_ref), (q_hbm, q_ref)]


def edge_kernel(group_hbm, doc_hbm, q_hbm, k_hbm, v_hbm, key_ref, value_ref, group_ref, *refs):
    *refs, sem = refs
    extra = (key_ref.shape[0] - value_ref.shape[0]) // 2
    near, rest = key_ref.shape[0] - extra, value_ref.shape[0]
    pairs = [(last_rows(k_hbm, near), key_ref.at[pl.ds(0, near)]), (last_rows(v_hbm, rest), value_ref),
             (v_hbm.at[pl.ds(v_hbm.shape[0] - near, extra)], key_ref.at[pl.ds(near, extra)])]

    me = flat_index()

    @pl.when((me % 2 == 1) | (me == 0))
    def _():
        copies = [pltpu.make_async_copy(a, b, sem.at[i]) for i, (a, b) in enumerate(pairs)]
        for copy in copies:
            copy.start()

        @pl.when(first_pair())
        def _():
            run_all([(group_hbm, group_ref)] + own_loads(doc_hbm, q_hbm, k_hbm, v_hbm, *refs), sem.at[pl.ds(len(pairs), 5)])

        for copy in copies:
            copy.wait()


def load_kernel(given, group_hbm, doc_hbm, q_hbm, k_hbm, v_hbm, *refs):
    edge_ref, group_ref, *refs, sem = refs[given:]
    loads = [(group_hbm, group_ref)] + own_loads(doc_hbm, q_hbm, k_hbm, v_hbm, *refs)
    if not given:
        run_all(edge_loads(k_hbm, v_hbm, edge_ref) + loads, sem)
        return

    @pl.when(first_pair())
    def _():
        edge_ref[:, :k_hbm.shape[1]] = refs[2][refs[2].shape[0] - edge_ref.shape[0]:]
        edge_ref[:, k_hbm.shape[1]:] = refs[3][refs[3].shape[0] - edge_ref.shape[0]:]

    @pl.when(jnp.logical_not(first_pair()))
    def _():
        run_all(edge_loads(k_hbm, v_hbm, edge_ref) + loads, sem)


def inner_kernel(near, hops, group_ref, other_ref, doc_ref, q_ref, k_ref, v_ref, bias_ref, local_ref, *out_ref):
    rows, width = q_ref.shape
    me = flat_index()
    own = doc_ref[pl.ds(me, 1), :]
    before = [doc_ref[pl.ds(jnp.maximum(me - j, 0), 1), :] for j in range(1, hops + 1)]
    col = column_of(own)
    t = lax.broadcasted_iota(jnp.int32, (rows, rows), 0)
    u = lax.broadcasted_iota(jnp.int32, (rows, rows), 1)
    if near == rows:
        seen = [(col == own) & (t <= u)]
        seen += [(column_of(before[j]) == own) & (t + (me - 1 - j) * rows >= 0) for j in range(hops)]
        seen = [bias_of(part) for part in seen]
    else:
        docs = column_of(jnp.where(lax.broadcasted_iota(jnp.int32, own.shape, 1) < near, own, before[0]))
        pos = jnp.where(t < near, t, t - rows)
        seen = [bias_of((docs == own) & (pos <= u) & (pos + me * rows >= 0))[:, :near]]
    tall = jnp.concatenate([jnp.concatenate(seen, axis=0)] * HEADS_DEV, axis=1)
    bias_ref[...] = tall[near:]
    first = q_ref.at[pl.ds(0, near)]
    for g in range(width // WIDTH):
        local_ref[g] = tall_scores(head_stack(first, g), k_ref[:near, columns((group_ref, other_ref), g)], tall[:near])
    if near < rows:
        bias = bias_of((own == col) & (u <= t))[near:]
        far = q_ref.at[pl.ds(near, rows - near)]
        for g in range(width // WIDTH):
            c = columns((group_ref, other_ref), g)
            scores = scores_of(head_stack(far, g), k_ref[:, c], bias)
            store_heads(out_ref[0], g, mix(*softmax_parts(scores), v_ref[:, c]))


def with_rim(own_ref, near, rims, small, group_ref, g, offset):
    here = columns(group_ref, g)
    if small:
        me = flat_index()
        *main, side = rims
        if offset:
            main = jnp.concatenate([main[0][near:, here], main[1][:, here]], axis=0)
        else:
            main = main[0][:near, here]
        parts = [jnp.where((me % 2 == 1) | (me == 0), side[:, columns(group_ref, g, offset)], main)]
    else:
        parts = [r[:, columns(group_ref, g, offset)] for r in rims]
    return jnp.concatenate(([] if own_ref is None else [own_ref[:near, here]]) + parts, axis=0)


def weight_kernel(small, group_ref, other_ref, q_ref, bias_ref, local_ref, *refs):
    *rims, weight_ref, inverse_ref = refs
    groups, near = q_ref.shape[1] // WIDTH, weight_ref.shape[1] // HEADS_DEV
    q_ref = q_ref.at[pl.ds(0, near)]
    rims = [with_rim(None, near, rims, small, (group_ref, other_ref), g, 0) for g in range(groups)]
    scores = [tall_scores(head_stack(q_ref, g), rims[g], bias_ref[...]) for g in range(groups)]
    scores = [jnp.concatenate([local_ref[g], scores[g]], axis=0) for g in range(groups)]
    totals = []
    for g in range(groups):
        expo = jnp.exp2(scores[g] - jnp.max(scores[g], axis=0, keepdims=True))
        weight_ref[g] = jnp.transpose(expo.astype(jnp.bfloat16))
        totals.append(jnp.sum(expo, axis=0, keepdims=True))
    spare = inverse_ref.shape[1] - groups
    inverse = 1.0 / jnp.concatenate(totals, axis=0)
    inverse = jnp.concatenate([inverse, jnp.zeros((spare, inverse.shape[1]), jnp.float32)], axis=0) if spare else inverse
    inverse_ref[...] = jnp.transpose(inverse)


def mix_kernel(small, group_ref, other_ref, weight_ref, inverse_ref, v_ref, *refs):
    *rims, out_ref, buf, sem = refs
    groups = weight_ref.shape[0]
    if small:
        *rims, done_ref = rims
        far = pltpu.make_async_copy(done_ref, out_ref.at[pl.ds(buf.shape[0], done_ref.shape[0])], sem.at[groups])
        far.start()
    for g in range(groups):
        value = with_rim(v_ref, buf.shape[0], rims, small, (group_ref, other_ref), g, v_ref.shape[1])
        store_heads(buf, g, mix(weight_ref[g], inverse_ref[:, g:g + 1], value))
        send_out(buf, out_ref, 0, g, sem).start()
    for g in range(groups):
        send_out(buf, out_ref, 0, g, sem).wait()
    if small:
        far.wait()


SMEM = pl.BlockSpec(memory_space=pltpu.SMEM)
VMEM = pl.BlockSpec(memory_space=pltpu.VMEM)
ANY = pl.BlockSpec(memory_space=pl.ANY)


def cycles(devices, period):
    firsts = [0, period // 2 + 1] + [m - 1 for m in range(period, devices, period)] + [devices]
    pairs = []
    for a, b in zip(firsts, firsts[1:]):
        pairs += [(i, i + 1) for i in range(a, b - 1)] + [(b - 1, a)]
    return pairs


def on_device(queries, key_rows, value_rows, group_kv_head, doc_ids):
    rows, width = queries.shape
    devices = lax.axis_size("ctx") * lax.axis_size("head")
    period = 2 * lax.axis_size("head")
    groups = width // WIDTH
    reach = rows * lax.axis_size("head") // 8
    near = min(reach, rows)
    hops = -(-reach // rows)
    small = near < rows
    dtype = queries.dtype
    docs = doc_ids.reshape(devices, rows)
    vmem = lambda x: pltpu.with_memory_space_constraint(x, pltpu.VMEM) if small else x
    chip = pltpu.VMEM if small else jax.ShapeDtypeStruct
    keys = 2 * near if small else rows * (1 + hops)
    kv_shape = key_rows.shape
    sent, early, arguments = {}, [], (group_kv_head, docs, queries, key_rows, value_rows)
    tables = [chip(docs.shape, jnp.int32), chip(queries.shape, dtype), chip(kv_shape, dtype), chip(kv_shape, dtype)]
    names = pltpu.SMEM(group_kv_head.shape, jnp.int32)
    if small:
        extra = near // 4
        key_edge, value_edge, early_group, *early = pl.pallas_call(
            edge_kernel,
            out_shape=[chip((near + extra, kv_shape[1]), dtype), chip((near - extra, kv_shape[1]), dtype), names] + tables,
            in_specs=[ANY] * 5, out_specs=[VMEM] * 2 + [SMEM] + [VMEM] * 4, name="edges",
            scratch_shapes=[pltpu.SemaphoreType.DMA((8,))],
        )(*arguments)
        for name, array in (("main_k", key_edge), ("main_v", value_edge)):
            sent[name] = lax.ppermute(array, AXES, cycles(devices, period))
    edge, group, near_docs, q, k, v = pl.pallas_call(
        functools.partial(load_kernel, len(early)), out_shape=[chip((near, 2 * kv_shape[1]), dtype), names] + tables,
        in_specs=[ANY] * 5 + [VMEM] * len(early), out_specs=[VMEM, SMEM] + [VMEM] * 4, name="load",
        scratch_shapes=[pltpu.SemaphoreType.DMA((7,))],
        input_output_aliases={5 + i: 2 + i for i in range(len(early))},
    )(*arguments, *[vmem(x) for x in early])
    groups_of = (group, early_group if small else group)
    bias, local, *done = pl.pallas_call(
        functools.partial(inner_kernel, near, hops),
        out_shape=[chip((keys - near, HEADS_DEV * near), jnp.float32), chip((groups, near, HEADS_DEV * near), jnp.float32)]
        + [chip((rows - near, width), dtype)] * small,
        in_specs=[SMEM] * 2 + [VMEM] * 4, out_specs=[VMEM] * (2 + small), name="inner",
    )(*groups_of, *[vmem(x) for x in (near_docs, q, k, v)])
    if small:
        side = lax.ppermute(edge, AXES, [(i, i ^ 1) for i in range(devices)])
        key_rims, value_rims = [sent["main_k"], side], [sent["main_k"], sent["main_v"], side]
    else:
        key_rims = value_rims = [
            lax.ppermute(edge, AXES, [(i, i + j) for i in range(devices - j)]) for j in range(1, hops + 1)]
    stack = HEADS_DEV * near
    weights, inverse = pl.pallas_call(
        functools.partial(weight_kernel, small),
        out_shape=[chip((groups, stack, keys), dtype), chip((stack, -(-groups // 8) * 8), jnp.float32)],
        in_specs=[SMEM] * 2 + [VMEM] * (3 + len(key_rims)), out_specs=[VMEM] * 2, name="weights",
    )(*groups_of, *[vmem(x) for x in (q, bias, local, *key_rims)])
    ins = [vmem(x) for x in (weights, inverse, v, *value_rims, *done)]
    return pl.pallas_call(
        functools.partial(mix_kernel, small),
        out_shape=jax.ShapeDtypeStruct(queries.shape, dtype),
        in_specs=[SMEM] * 2 + [VMEM] * len(ins), out_specs=ANY, name="mix",
        scratch_shapes=[pltpu.VMEM((near, width), dtype), pltpu.SemaphoreType.DMA((groups + 1,))],
    )(*groups_of, *ins)


def solution(mesh):
    placed = P(AXES, None)
    return jax.shard_map(
        on_device, mesh=mesh, in_specs=(placed, placed, placed, P(), P()), out_specs=placed, check_vma=False
    )
```
